128 devices in a mesh: row: 8 (over x, z_hi), col: 16 (over z_lo, y, core).
Axes of the slice: x: 4, y: 4, z: 4 (z_hi: 2, z_lo: 2; z = z_hi * 2 + z_lo), core: 2. Of those that a mesh axis runs over, the one named last changes fastest.
Arguments:
- window: float32 [12288, 12288], P('row', 'col'), may hold values from -6 to 6
- reflectors: float32 [2, 12288, 256], P(None, 'row', 'col'), may hold values from -0.0546875 to 0.0546875
- factors: float32 [2, 256, 256], replicated, may hold values from -0.375 to 0.375
Outputs:
- updated: float32 [12288, 12288], P('row', 'col')
The draws below stay inside these ranges and needn't reach their ends.
All inputs are finite; a program needn't handle non-finite values.
Results may differ from the reference program's by a relative error of at most 0.0001.
Values sent between devices are 32-bit elements; how exact they have to be, the bound alone decides.
A program may use at most 128 MiB of HBM per device.

```python
import jax
import jax.numpy as jnp
from jax import lax

N = 12288
B = 256
PANELS = 2


def block_levels(key, dims, shards, least, largest):
    level = 1.0
    for dim, blocks in shards:
        steps = jax.random.uniform(jax.random.fold_in(jax.random.fold_in(key, 6), dim), (blocks,), jnp.float32, least / len(shards), largest / len(shards))
        level = level * jnp.repeat(jnp.exp(steps), dims[dim] // blocks).reshape((-1,) + (1,) * (len(dims) - 1 - dim))
    return level


def gaussian(own_key, dims, spread, bound, pieces=(), held_as=jnp.bfloat16):
    level = block_levels(own_key, dims, pieces, -0.22, 0.18) if pieces else 1.0
    result = jax.random.normal(own_key, dims, jnp.float32) * spread * level
    return jnp.minimum(jnp.maximum(result, -bound), bound).astype(held_as)


def setup_inputs(seed: int = 0) -> dict:
    streams_of = jax.random.split(jax.random.key(seed), 4)
    window = gaussian(streams_of[0], (N, N), 1.0, 6.0, ((0, 8), (1, 16)), jnp.float32)
    reflectors = gaussian(streams_of[1], (PANELS, N, B), N ** -0.5, 0.0546875, ((1, 8), (2, 16)), jnp.float32)
    factors = gaussian(streams_of[2], (PANELS, B, B), B ** -0.5, 0.375, (), jnp.float32)
    return {"window": window, "reflectors": reflectors, "factors": factors}


highest = lax.Precision.HIGHEST


def product(factor_one, factor_two):
    return jnp.dot(factor_one, factor_two, precision=highest, preferred_element_type=jnp.float32)


def reference(window, reflectors, factors):
    updated = window
    for panel in range(PANELS):
        vectors = reflectors[panel]
        factor = factors[panel]
        projected = product(vectors.T, updated)
        updated = updated - product(vectors, product(factor.T, projected))
        image = product(updated, vectors)
        updated = updated - product(product(image, factor), vectors.T)
    return updated
```

```python
import jax
import jax.numpy as jnp
from jax import lax
from jax.sharding import PartitionSpec as P

HIGH = lax.Precision.HIGH


def mm(a, b, ca, cb):
    return lax.dot_general(a, b, (((ca,), (cb,)), ((), ())), precision=HIGH, preferred_element_type=jnp.float32)


def body(window, reflectors, factors):
    panels, rows, piece = reflectors.shape
    cols = window.shape[1]
    row_n = lax.axis_size("row")
    col_n = lax.axis_size("col")
    block = piece * col_n
    width = panels * block
    c = lax.axis_index("col")
    vt = jnp.swapaxes(reflectors, 1, 2)
    vr = lax.all_gather(vt, "col", axis=1, tiled=True).reshape(width, rows)
    halves = vt.reshape(panels, piece, 2, cols)
    k = c % 2
    own = lax.dynamic_index_in_dim(halves, k, 2, keepdims=False)
    other = lax.dynamic_index_in_dim(halves, 1 - k, 2, keepdims=False)
    pairs_a = []
    pairs_b = []
    for r in range(row_n):
        for cc in range(col_n):
            pairs_a.append((r * col_n + cc, (cc // 2) * col_n + 2 * r + cc % 2))
            pairs_b.append((r * col_n + cc, (cc // 2) * col_n + 2 * r + 1 - cc % 2))
    got_a = lax.ppermute(own, ("row", "col"), pairs_a)
    got_b = lax.ppermute(other, ("row", "col"), pairs_b)
    first = jnp.where(k == 0, got_a, got_b)
    second = jnp.where(k == 0, got_b, got_a)
    pair = jnp.stack([first, second], 1)
    vc = lax.all_gather(pair, "row", axis=1, tiled=True).reshape(width, cols)

    p_part = mm(vr, window, 1, 0)
    y_part = mm(window, vc, 1, 1)
    p_own = lax.psum_scatter(p_part, "row", scatter_dimension=0, tiled=True)
    y_own = lax.psum_scatter(y_part, "col", scatter_dimension=0, tiled=True)
    g12 = lax.psum(mm(vc[:block], vc[block:], 1, 1), "col")
    s_own = lax.psum(mm(p_own, vc, 1, 1), "col")
    t1, t2 = factors[0], factors[1]
    t12 = -mm(mm(t1, g12, 1, 0), t2, 1, 0)
    tc = jnp.concatenate([jnp.concatenate([t1, t12], 1), jnp.concatenate([jnp.zeros_like(t1), t2], 1)], 0)
    p_own = p_own - mm(mm(s_own, tc, 1, 0), vc, 1, 0)
    z_own = mm(y_own, tc, 1, 0)
    p_all = lax.all_gather(p_own, "row", axis=0, tiled=True)
    z_all = lax.all_gather(z_own, "col", axis=0, tiled=True)
    q = mm(tc, p_all, 0, 0)
    return window - mm(vr, q, 0, 0) - mm(z_all, vc, 1, 0)


def solution(mesh):
    placed = (P("row", "col"), P(None, "row", "col"), P())
    return jax.shard_map(body, mesh=mesh, in_specs=placed, out_specs=P("row", "col"), check_vma=False)
```

```python
import jax
import jax.numpy as jnp
from jax import lax
from jax.experimental import pallas as pl
from jax.experimental.pallas import tpu as pltpu
from jax.sharding import PartitionSpec as P

MESH = pl.DeviceIdType.MESH
F32 = jnp.float32
HIGH = lax.Precision.HIGH


def mm(a, b, ca, cb):
    return lax.dot_general(a, b, (((ca,), (cb,)), ((), ())), precision=HIGH, preferred_element_type=F32)


def remote(src, dst, ssem, rsem, dev):
    return pltpu.make_async_remote_copy(
        src_ref=src, dst_ref=dst, send_sem=ssem, recv_sem=rsem, device_id=dev, device_id_type=MESH
    )


def landed(ref, sem):
    pltpu.make_async_copy(ref, ref, sem).wait()


class Gather:
    def __init__(self, own, place, ring, pair, core, ssem, rsem):
        self.own, self.place, self.ring, self.pair, self.core = own, place, ring, pair, core
        self.ssem, self.rsem, self.started = ssem, rsem, []

    def send(self, src, dst, slot, dev):
        copy = remote(src, dst, self.ssem.at[len(self.started)], self.rsem.at[slot], dev)
        copy.start()
        self.started.append(copy)

    def start(self):
        place = self.place(0, 0, 0)
        self.send(self.own, place, 4, self.pair)
        for d in (1, 3, 2):
            self.send(self.own, place, d, self.ring(d))
        if self.core is not None:
            self.send(self.own, place, 8, self.core)

    def wait(self, level, d, other=0):
        landed(self.place(level, d, other), self.rsem.at[other * 8 + level * 4 + d])

    def to_core(self, level, d):
        place = self.place(level, d, 0)
        self.send(place, place, 8 + level * 4 + d, self.core)

    def relay_pair(self):
        self.wait(1, 0)
        place = self.place(1, 0, 0)
        for d in (1, 3, 2):
            self.send(place, place, 4 + d, self.ring(d))
        if self.core is not None:
            self.to_core(1, 0)

    def take_ring(self, level):
        for d in (1, 3, 2):
            self.wait(level, d)
            if self.core is not None:
                self.to_core(level, d)

    def take_core(self, level):
        for d in (0, 1, 3, 2):
            self.wait(level, d, 1)

    def finish(self):
        for copy in self.started:
            copy.wait_send()


def kernel(
    w_hbm, v_hbm, t_hbm, out_hbm,
    w, vr, vc, tf, tc, vv,
    p, p_rx, p_acc, p_pair, p_own, p_all,
    y_send, y_core, y_own, y_rx, y_acc, y_pair, z_all,
    g_part, g_rx, g_own, g_all, s_part, s_rx, s_own, s_all,
    load_sem, zero_s, zero_r, vr_s, vr_r, vc_s, vc_r, pa_s, pa_r, za_s, za_r,
    p_s, p_r, pz_s, pz_r, yc_s, yc_r, y_s, y_r, yz_s, yz_r,
    g_s, g_r, out_sem,
):
    r = lax.axis_index("row")
    c = lax.axis_index("col")
    x, zh = r // 2, r % 2
    zl, y, k = c // 8, (c // 2) % 4, c % 2

    def dev(x_, zh_, zl_, y_, k_):
        return (x_ * 2 + zh_, (zl_ * 4 + y_) * 2 + k_)

    def ring_x(d):
        return dev((x + d) % 4, zh, zl, y, k)

    def ring_y(d):
        return dev(x, zh, zl, (y + d) % 4, k)

    pair_x = dev(x, 1 - zh, zl, y, k)
    pair_y = dev(x, zh, 1 - zl, y, k)
    core = dev(x, zh, zl, y, 1 - k)

    def level_of(z, level):
        return z if level == 0 else 1 - z

    def col_index(level, d, other):
        return (level_of(zl, level) * 4 + (y + 4 - d) % 4) * 2 + level_of(k, other)

    def row_index(level, d):
        return ((x + 4 - d) % 4) * 2 + level_of(zh, level)

    def z_index(level, d, other):
        return level_of(k, other) * 8 + level_of(zl, level) * 4 + (y + 4 - d) % 4

    gather_vr = Gather(v_hbm, lambda l, d, o: vr.at[:, col_index(l, d, o)], ring_y, pair_y, core, vr_s, vr_r)
    gather_vr.start()
    halves = []
    for h in range(2):
        src = v_hbm.at[:, :, pl.ds(h * 768, 768)]
        at_home = jnp.logical_and(c // 2 == r, k == h)
        away = jnp.logical_not(at_home)
        local = pltpu.make_async_copy(src, vc.at[:, c], zero_r.at[k])
        far = remote(src, vc.at[:, c], zero_s.at[h], zero_r.at[k], (c // 2, 2 * r + h))
        pl.when(at_home)(local.start)
        pl.when(away)(far.start)
        halves.append((away, far))
    own_v = pltpu.make_async_copy(v_hbm, vr.at[:, c], load_sem.at[0])
    own_v.start()
    load_w = pltpu.make_async_copy(w_hbm, w, load_sem.at[1])
    load_w.start()
    load_t = pltpu.make_async_copy(t_hbm, tf, load_sem.at[2])
    load_t.start()

    mine = vc.at[:, pl.ds(2 * r, 2)]
    gather_vc = Gather(
        mine, lambda l, d, o: vc.at[:, pl.ds(2 * row_index(l, d), 2)], ring_x, pair_x, None, vc_s, vc_r
    )
    gather_vr.relay_pair()
    for kk in range(2):
        landed(vc.at[:, 2 * r + kk], zero_r.at[kk])
    gather_vc.start()
    gather_vr.take_ring(0)
    gather_vc.relay_pair()
    own_v.wait()
    load_w.wait()
    load_t.wait()
    gather_vr.take_ring(1)
    gather_vr.take_core(0)
    gather_vr.take_core(1)

    g_part[...] = mm(vr[0, c], vr[1].reshape(256, 1536), 1, 1)

    def g_send(i, _):
        pltpu_copy = remote(g_part, g_rx.at[i], g_s.at[0], g_r.at[0], ((r + 1 + i) % 8, c))
        pltpu_copy.start()
        return 0

    lax.fori_loop(0, 7, g_send, 0)
    p_copies = []
    for n in range(3):
        p[n] = mm(vr[...].reshape(512, 1536), w[:, n * 256:(n + 1) * 256], 1, 0).reshape(4, 2, 64, 256)
        for d in (2, 1, 3):
            copy = remote(
                p.at[n, (x + d) % 4], p_rx.at[n, d - 1], p_s.at[n, d - 1], p_r.at[n, d - 1], ring_x(d)
            )
            copy.start()
            p_copies.append(copy)

    gather_vc.take_ring(0)
    gather_vc.take_ring(1)

    def y_tile(row):
        rows = pl.ds(pl.multiple_of(row, 384), 384)
        return mm(w[rows, :], vc[...].reshape(512, 768), 1, 1)

    y_copies = []
    for t in range(2):
        y_send[t] = y_tile((1 - k) * 768 + t * 384)
        copy = remote(y_send.at[t], y_core.at[t], yc_s.at[t], yc_r.at[t], core)
        copy.start()
        y_copies.append(copy)
    for t in range(2):
        part = y_tile(k * 768 + t * 384)
        landed(y_core.at[t], yc_r.at[t])
        y_own[t] = (part + y_core[t]).reshape(4, 96, 512)
        for d in (2, 1, 3):
            copy = remote(
                y_own.at[t, (y + d) % 4], y_rx.at[t, d - 1], y_s.at[t, d - 1], y_r.at[t, d - 1], ring_y(d)
            )
            copy.start()
            y_copies.append(copy)

    landed(g_rx, g_r.at[0])
    g_own[...] = (g_part[...] + g_rx[0] + g_rx[1] + g_rx[2]) + (g_rx[3] + g_rx[4] + g_rx[5] + g_rx[6])
    g_all[c] = g_own[...]

    def g_spread(i, _):
        remote(g_own, g_all.at[c], g_s.at[1], g_r.at[1], (r, (c + 1 + i) % 16)).start()
        return 0

    lax.fori_loop(0, 15, g_spread, 0)

    for n in range(3):
        for d in range(3):
            landed(p_rx.at[n, d], p_r.at[n, d])
        p_acc[n] = (p[n, x] + p_rx[n, 0]) + (p_rx[n, 1] + p_rx[n, 2])
        copy = remote(p_acc.at[n, 1 - zh], p_pair.at[n], pz_s.at[n], pz_r.at[n], pair_x)
        copy.start()
        p_copies.append(copy)
    for n in range(3):
        landed(p_pair.at[n], pz_r.at[n])
        p_own[:, n * 256:(n + 1) * 256] = p_acc[n, zh] + p_pair[n]

    part = mm(p_own[...], vc[...].reshape(512, 768), 1, 1)
    s_part[0] = part[:, :256]
    s_part[1] = part[:, 256:]

    def chunk(ref, who):
        return ref.at[who % 2, pl.ds(pl.multiple_of(who // 2 * 8, 8), 8)]

    def s_send(i, _):
        to = (c + 1 + i) % 16
        remote(chunk(s_part, to), s_rx.at[i], g_s.at[2], g_r.at[2], (r, to)).start()
        return 0

    lax.fori_loop(0, 15, s_send, 0)

    for t in range(2):
        for d in range(3):
            landed(y_rx.at[t, d], y_r.at[t, d])
        y_acc[t] = (y_own[t, y] + y_rx[t, 0]) + (y_rx[t, 1] + y_rx[t, 2])
    copy = remote(y_acc.at[1 - zl], y_pair, yz_s.at[0], yz_r.at[0], pair_y)
    copy.start()
    y_copies.append(copy)

    landed(s_rx, g_r.at[2])
    total = s_part[k, pl.ds(pl.multiple_of(c // 2 * 8, 8), 8)]
    for i in range(15):
        total = total + s_rx[i]
    s_own[...] = total
    s_all[k, pl.ds(pl.multiple_of(c // 2 * 8, 8), 8)] = total

    def s_spread(i, _):
        remote(s_own, chunk(s_all, c), g_s.at[3], g_r.at[3], (r, (c + 1 + i) % 16)).start()
        return 0

    lax.fori_loop(0, 15, s_spread, 0)

    landed(g_all.at[pl.ds(0, 15)], g_r.at[1])
    tc[0:256, 0:256] = tf[0]
    tc[256:512, 256:512] = tf[1]
    tc[256:512, 0:256] = jnp.zeros((256, 256), F32)
    tc[0:256, 256:512] = -mm(mm(tf[0], g_all[...].reshape(256, 256), 1, 0), tf[1], 1, 0)

    landed(y_pair, yz_r.at[0])
    z_place = lambda l, d, o: z_all.at[z_index(l, d, o)]
    z_all[z_index(0, 0, 0)] = mm(y_acc[zl] + y_pair[...], tc[...], 1, 0)
    gather_z = Gather(z_place(0, 0, 0), z_place, ring_y, pair_y, core, za_s, za_r)
    gather_z.start()

    landed(s_rx, g_r.at[3])
    s_rows = jnp.concatenate([s_all[0], s_all[1]], axis=1)
    p_all[r] = p_own[...] - mm(mm(s_rows, tc[...], 1, 0), vc[...].reshape(512, 768), 1, 0)
    p_place = lambda l, d, o: p_all.at[row_index(l, d)]
    gather_p = Gather(p_place(0, 0, 0), p_place, ring_x, pair_x, None, pa_s, pa_r)
    gather_p.start()

    def vv_tile(i):
        cols = slice(i * 512, (i + 1) * 512)
        vv[:, cols] = mm(tc[...], vr[...].reshape(512, 1536)[:, cols], 1, 0)

    gather_z.relay_pair()
    gather_p.relay_pair()
    for i in range(3):
        vv_tile(i)

    def z_tile(level, other):
        first = level_of(k, other) * 8 + level_of(zl, level) * 4
        rows = pl.ds(pl.multiple_of(first * 96, 384), 384)
        w[rows, :] = w[rows, :] - mm(z_all[pl.ds(first, 4)].reshape(384, 512), vc[...].reshape(512, 768), 1, 0)

    gather_z.take_ring(0)
    z_tile(0, 0)
    gather_z.take_ring(1)
    z_tile(1, 0)
    gather_z.take_core(0)
    z_tile(0, 1)
    gather_z.take_core(1)
    z_tile(1, 1)
    gather_p.take_ring(0)
    gather_p.take_ring(1)

    outs = []
    for i in range(4):
        rows = slice(i * 384, (i + 1) * 384)
        w[rows, :] = w[rows, :] - mm(vv[:, rows], p_all[...].reshape(512, 768), 0, 0)
        copy = pltpu.make_async_copy(w.at[pl.ds(i * 384, 384)], out_hbm.at[pl.ds(i * 384, 384)], out_sem.at[i])
        copy.start()
        outs.append(copy)

    for away, far in halves:
        pl.when(away)(far.wait_send)
    for gather in (gather_vr, gather_vc, gather_z, gather_p):
        gather.finish()
    for copy in p_copies + y_copies:
        copy.wait_send()
    landed(g_rx, g_s.at[0])
    landed(g_all.at[pl.ds(0, 15)], g_s.at[1])
    landed(s_rx, g_s.at[2])
    landed(s_rx, g_s.at[3])
    for copy in outs:
        copy.wait()


def body(window, reflectors, factors):
    vt = jnp.swapaxes(reflectors, 1, 2)
    dma = pltpu.SemaphoreType.DMA
    vmem = lambda *s: pltpu.VMEM(s, F32)
    return pl.pallas_call(
        kernel,
        out_shape=jax.ShapeDtypeStruct(window.shape, F32),
        in_specs=[pl.BlockSpec(memory_space=pl.ANY)] * 3,
        out_specs=pl.BlockSpec(memory_space=pl.ANY),
        scratch_shapes=[
            vmem(1536, 768), vmem(2, 16, 16, 1536), vmem(2, 16, 16, 768), vmem(2, 256, 256), vmem(512, 512),
            vmem(512, 1536),
            vmem(3, 4, 2, 64, 256), vmem(3, 3, 2, 64, 256), vmem(3, 2, 64, 256), vmem(3, 64, 256), vmem(64, 768),
            vmem(8, 64, 768),
            vmem(2, 384, 512), vmem(2, 384, 512), vmem(2, 4, 96, 512), vmem(2, 3, 96, 512), vmem(2, 96, 512),
            vmem(96, 512), vmem(16, 96, 512),
            vmem(16, 256), vmem(7, 16, 256), vmem(16, 256), vmem(16, 16, 256),
            vmem(2, 64, 256), vmem(15, 8, 256), vmem(8, 256), vmem(2, 64, 256),
            dma((3,)), dma((2,)), dma((2,)), dma((15,)), dma((16,)), dma((7,)), dma((8,)), dma((7,)), dma((8,)),
            dma((15,)), dma((16,)),
            dma((3, 3)), dma((3, 3)), dma((3,)), dma((3,)), dma((2,)), dma((2,)), dma((2, 3)), dma((2, 3)),
            dma((1,)), dma((1,)),
            dma((4,)), dma((4,)), dma((4,)),
        ],
        compiler_params=pltpu.CompilerParams(has_side_effects=True, vmem_limit_bytes=60 * 1024 * 1024),
    )(window, vt, factors)


def solution(mesh):
    placed = (P("row", "col"), P(None, "row", "col"), P())
    return jax.shard_map(body, mesh=mesh, in_specs=placed, out_specs=P("row", "col"), check_vma=False)
```

```python
import jax
import jax.numpy as jnp
from jax import lax
from jax.experimental import pallas as pl
from jax.experimental.pallas import tpu as pltpu
from jax.sharding import PartitionSpec as P

MESH = pl.DeviceIdType.MESH
F32 = jnp.float32
HIGH = lax.Precision.HIGH


def mm(a, b, ca, cb):
    return lax.dot_general(a, b, (((ca,), (cb,)), ((), ())), precision=HIGH, preferred_element_type=F32)


def remote(src, dst, ssem, rsem, dev):
    return pltpu.make_async_remote_copy(
        src_ref=src, dst_ref=dst, send_sem=ssem, recv_sem=rsem, device_id=dev, device_id_type=MESH
    )


def landed(ref, sem):
    pltpu.make_async_copy(ref, ref, sem).wait()


class Sends:
    def __init__(self, ssem):
        self.ssem, self.started = ssem, []

    def __call__(self, src, dst, rsem, dev):
        copy = remote(src, dst, self.ssem.at[len(self.started)], rsem, dev)
        copy.start()
        self.started.append(copy)

    def finish(self):
        for copy in self.started:
            copy.wait_send()


class Gather:
    def __init__(self, own, place, ring, pair, core, send, rsem):
        self.own, self.place, self.ring, self.pair, self.core = own, place, ring, pair, core
        self.send, self.rsem = send, rsem

    def sem(self, level, d, q, other=0):
        return self.rsem.at[other * 16 + level * 8 + d * 2 + q]

    def start(self):
        for q in (0, 1):
            self.send(self.own(q), self.place(0, 0, 0, q), self.sem(1, 0, q), self.pair)
            self.send(self.own(q), self.place(0, 0, 0, q), self.sem(0, 1, q), self.ring(1))
            self.send(self.own(1 - q), self.place(0, 0, 0, 1 - q), self.sem(0, 3, 1 - q), self.ring(3))
        if self.core is not None:
            for q in (0, 1):
                self.send(self.own(q), self.place(0, 0, 0, q), self.sem(0, 0, q, 1), self.core)

    def wait(self, level, d, q, other=0):
        landed(self.place(level, d, other, q), self.sem(level, d, q, other))

    def to_core(self, level, d, q):
        if self.core is not None:
            place = self.place(level, d, 0, q)
            self.send(place, place, self.sem(level, d, q, 1), self.core)

    def hand_on(self, level):
        for d, q, to in ((1, 0, 1), (3, 1, 3)):
            self.wait(level, d, q)
            place = self.place(level, d, 0, q)
            self.send(place, place, self.sem(level, 2, q), self.ring(to))
            self.to_core(level, d, q)

    def relay_pair(self):
        for q in (0, 1):
            self.wait(1, 0, q)
            place = self.place(1, 0, 0, q)
            self.send(place, place, self.sem(1, 1, q), self.ring(1))
            self.send(place, place, self.sem(1, 3, q), self.ring(3))
            self.to_core(1, 0, q)

    def take_near(self, level):
        for d, q in ((1, 1), (3, 0)):
            self.wait(level, d, q)
            self.to_core(level, d, q)

    def take_far(self, level):
        for q in (0, 1):
            self.wait(level, 2, q)
            self.to_core(level, 2, q)

    def take_core(self, level):
        for d in (0, 1, 3, 2):
            for q in (0, 1):
                self.wait(level, d, q, 1)


def kernel(
    w_hbm, v_hbm, t_hbm, w, vv, p_all,
    vr, vc, tf, tc,
    p, p_far, p_rx, p_acc, p_pair, p_own,
    y_send, y_core, y_own, y_far, y_rx, y_acc, y_pair, z_all,
    g_part, g_rx, g_own, g_all, s_part, s_rx, s_own, s_all,
    load_sem, zero_s, zero_r, all_s, vr_r, vc_r, pa_r, za_r,
    pf_r, p_r, pz_r, yc_r, yf_r, y_r, yz_r, g_s, g_r,
):
    r = lax.axis_index("row")
    c = lax.axis_index("col")
    x, zh = r // 2, r % 2
    zl, y, k = c // 8, (c // 2) % 4, c % 2

    def dev(x_, zh_, zl_, y_, k_):
        return (x_ * 2 + zh_, (zl_ * 4 + y_) * 2 + k_)

    def ring_x(d):
        return dev((x + d) % 4, zh, zl, y, k)

    def ring_y(d):
        return dev(x, zh, zl, (y + d) % 4, k)

    pair_x = dev(x, 1 - zh, zl, y, k)
    pair_y = dev(x, zh, 1 - zl, y, k)
    core = dev(x, zh, zl, y, 1 - k)

    def level_of(z, level):
        return z if level == 0 else 1 - z

    def col_index(level, d, other):
        return (level_of(zl, level) * 4 + (y + 4 - d) % 4) * 2 + level_of(k, other)

    def row_index(level, d):
        return ((x + 4 - d) % 4) * 2 + level_of(zh, level)

    def vc_pair(level, d):
        other_x = (x + 4 - d) % 4
        return (level_of(zh, level) + c // 2) % 2 * 4 + (other_x + 4 - c // 4) % 4

    def z_index(level, d, other):
        return level_of(k, other) * 8 + level_of(zl, level) * 4 + (y + 4 - d) % 4

    load_w = pltpu.make_async_copy(w_hbm, w, load_sem.at[1])
    load_w.start()
    own_v = pltpu.make_async_copy(v_hbm, vr.at[:, c], load_sem.at[0])
    own_v.start()
    load_t = pltpu.make_async_copy(t_hbm, tf, load_sem.at[2])
    load_t.start()

    target = (x + y) % 4 * 2 + (zh + zl) % 2
    share = vc_pair(0, 0)
    barrier = pltpu.get_barrier_semaphore()

    def greet(device):
        pl.semaphore_signal(barrier, inc=1, device_id=device, device_id_type=MESH)

    for h in range(2):
        apart = jnp.logical_not(jnp.logical_and(target == r, 2 * r + h == c))
        pl.when(apart)(lambda h=h: greet((target, 2 * r + h)))
        apart = jnp.logical_not(jnp.logical_and(c // 2 == r, 2 * share + h == c))
        pl.when(apart)(lambda h=h: greet((c // 2, 2 * share + h)))
    for device in (ring_x(1), ring_x(3), ring_y(1), ring_y(3), pair_x, pair_y, core):
        greet(device)
    home = jnp.logical_and(r == 0, c // 2 == 0)
    pl.semaphore_wait(barrier, 11 - 2 * home.astype(jnp.int32))

    halves = []
    for h in range(2):
        src = v_hbm.at[:, :, pl.ds(h * 768, 768)]
        at_home = jnp.logical_and(target == r, 2 * r + h == c)
        away = jnp.logical_not(at_home)
        local = pltpu.make_async_copy(src, vc.at[:, c], zero_r.at[k])
        far = remote(src, vc.at[:, c], zero_s.at[h], zero_r.at[k], (target, 2 * r + h))
        pl.when(at_home)(local.start)
        pl.when(away)(far.start)
        halves.append((away, far))
    send = Sends(all_s)
    gather_vr = Gather(
        lambda q: v_hbm.at[q], lambda l, d, o, q: vr.at[q, col_index(l, d, o)], ring_y, pair_y, core, send, vr_r
    )
    gather_vr.start()
    vc_place = lambda l, d, o, q: vc.at[q, pl.ds(2 * vc_pair(l, d), 2)]
    gather_vc = Gather(lambda q: vc_place(0, 0, 0, q), vc_place, ring_x, pair_x, None, send, vc_r)

    gather_vr.hand_on(0)
    for kk in range(2):
        landed(vc.at[:, 2 * share + kk], zero_r.at[kk])
    gather_vc.start()
    gather_vr.relay_pair()
    gather_vr.take_near(0)
    gather_vc.hand_on(0)
    gather_vr.hand_on(1)
    gather_vr.take_far(0)
    gather_vc.relay_pair()
    own_v.wait()
    load_w.wait()
    load_t.wait()
    gather_vr.take_near(1)
    gather_vr.take_core(0)

    def p_tile(m):
        rows = vr[:, pl.ds(level_of(zl, m) * 8, 8)].reshape(256, 1536)
        p[m] = mm(rows, w[...], 1, 0).reshape(4, 2, 32, 768)
        right, left, far = (x + 1) % 4, (x + 3) % 4, (x + 2) % 4
        send(p.at[m, far, 0], p_far.at[m, 0], pf_r.at[m, 0], ring_x(1))
        send(p.at[m, far, 1], p_far.at[m, 1], pf_r.at[m, 1], ring_x(3))
        send(p.at[m, right, 1], p_rx.at[m, 0], p_r.at[m, 0], ring_x(1))
        send(p.at[m, left, 0], p_rx.at[m, 1], p_r.at[m, 1], ring_x(3))

    def p_hand_on(m):
        right, left = (x + 1) % 4, (x + 3) % 4
        landed(p_far.at[m, 0], pf_r.at[m, 0])
        p[m, right, 0] = p[m, right, 0] + p_far[m, 0]
        send(p.at[m, right, 0], p_rx.at[m, 2], p_r.at[m, 2], ring_x(1))
        landed(p_far.at[m, 1], pf_r.at[m, 1])
        p[m, left, 1] = p[m, left, 1] + p_far[m, 1]
        send(p.at[m, left, 1], p_rx.at[m, 3], p_r.at[m, 3], ring_x(3))

    def p_sum(m):
        for i in range(4):
            landed(p_rx.at[m, i], p_r.at[m, i])
        p_acc[m, 0] = p[m, x, 0] + (p_rx[m, 1] + p_rx[m, 2])
        p_acc[m, 1] = p[m, x, 1] + (p_rx[m, 0] + p_rx[m, 3])
        send(p_acc.at[m, 1 - zh], p_pair.at[m], pz_r.at[m], pair_x)

    def p_take(m):
        landed(p_pair.at[m], pz_r.at[m])
        p_own[pl.ds(pl.multiple_of(level_of(zl, m) * 32, 32), 32), :] = p_acc[m, zh] + p_pair[m]

    def y_tile(row):
        rows = pl.ds(pl.multiple_of(row, 384), 384)
        return mm(w[rows, :], vc[...].reshape(512, 768), 1, 1)

    def y_other(t):
        y_send[t] = y_tile((1 - k) * 768 + t * 384)
        send(y_send.at[t], y_core.at[t], yc_r.at[t], core)

    def y_mine(t):
        part = y_tile(k * 768 + t * 384)
        landed(y_core.at[t], yc_r.at[t])
        y_own[t] = (part + y_core[t]).reshape(4, 96, 512)
        ahead, behind = (1, 3) if t == 0 else (3, 1)
        send(y_own.at[t, (y + 2) % 4], y_far.at[t], yf_r.at[t], ring_y(ahead))
        send(y_own.at[t, (y + behind) % 4], y_rx.at[t, 1], y_r.at[t, 1], ring_y(behind))

    def y_hand_on(t):
        ahead = 1 if t == 0 else 3
        to = (y + ahead) % 4
        landed(y_far.at[t], yf_r.at[t])
        y_own[t, to] = y_own[t, to] + y_far[t]
        send(y_own.at[t, to], y_rx.at[t, 0], y_r.at[t, 0], ring_y(ahead))

    def y_sum(t):
        landed(y_rx.at[t, 0], y_r.at[t, 0])
        landed(y_rx.at[t, 1], y_r.at[t, 1])
        y_acc[t] = y_own[t, y] + (y_rx[t, 0] + y_rx[t, 1])

    p_tile(0)
    gather_vc.hand_on(1)
    gather_vr.take_far(1)
    gather_vr.take_core(1)
    p_tile(1)
    g_part[...] = mm(vr[0, c], vr[1].reshape(256, 1536), 1, 1)
    gather_vc.take_near(0)
    gather_vc.take_far(0)
    gather_vc.take_near(1)
    gather_vc.take_far(1)
    p_hand_on(0)

    def g_send(i, _):
        remote(g_part, g_rx.at[i], g_s.at[0], g_r.at[0], ((r + 1 + i) % 8, c)).start()
        return 0

    lax.fori_loop(0, 7, g_send, 0)
    y_other(0)
    y_other(1)
    p_hand_on(1)
    y_mine(0)
    p_sum(0)
    y_mine(1)
    y_hand_on(0)
    p_sum(1)

    landed(g_rx, g_r.at[0])
    g_own[...] = (g_part[...] + g_rx[0] + g_rx[1] + g_rx[2]) + (g_rx[3] + g_rx[4] + g_rx[5] + g_rx[6])
    g_all[c] = g_own[...]

    def g_spread(i, _):
        remote(g_own, g_all.at[c], g_s.at[1], g_r.at[1], (r, (c + 1 + i) % 16)).start()
        return 0

    lax.fori_loop(0, 15, g_spread, 0)
    y_hand_on(1)
    p_take(0)
    p_take(1)

    part = mm(p_own[...], vc[...].reshape(512, 768), 1, 1)
    s_part[0] = part[:, :256]
    s_part[1] = part[:, 256:]

    def chunk(ref, who):
        return ref.at[who % 2, pl.ds(pl.multiple_of(who // 2 * 8, 8), 8)]

    def s_send(i, _):
        to = (c + 1 + i) % 16
        remote(chunk(s_part, to), s_rx.at[i], g_s.at[2], g_r.at[2], (r, to)).start()
        return 0

    lax.fori_loop(0, 15, s_send, 0)
    y_sum(0)
    y_sum(1)
    send(y_acc.at[1 - zl], y_pair, yz_r.at[0], pair_y)

    landed(g_all.at[pl.ds(0, 15)], g_r.at[1])
    tc[0:256, 0:256] = tf[0]
    tc[256:512, 256:512] = tf[1]
    tc[256:512, 0:256] = jnp.zeros((256, 256), F32)
    tc[0:256, 256:512] = -mm(mm(tf[0], g_all[...].reshape(256, 256), 1, 0), tf[1], 1, 0)

    landed(s_rx, g_r.at[2])
    total = s_part[k, pl.ds(pl.multiple_of(c // 2 * 8, 8), 8)]
    for i in range(15):
        total = total + s_rx[i]
    s_own[...] = total
    s_all[k, pl.ds(pl.multiple_of(c // 2 * 8, 8), 8)] = total

    def s_spread(i, _):
        remote(s_own, chunk(s_all, c), g_s.at[3], g_r.at[3], (r, (c + 1 + i) % 16)).start()
        return 0

    lax.fori_loop(0, 15, s_spread, 0)

    landed(y_pair, yz_r.at[0])
    z_place = lambda l, d, o, q: z_all.at[z_index(l, d, o), pl.ds(q * 48, 48)]
    z_all[z_index(0, 0, 0)] = mm(y_acc[zl] + y_pair[...], tc[...], 1, 0)
    gather_z = Gather(lambda q: z_place(0, 0, 0, q), z_place, ring_y, pair_y, core, send, za_r)
    gather_z.start()

    landed(s_rx, g_r.at[3])
    s_rows = jnp.concatenate([s_all[0], s_all[1]], axis=1)
    mine = p_own[...] - mm(mm(s_rows, tc[...], 1, 0), vc[...].reshape(512, 768), 1, 0)

    def p_place(l, d, o, q):
        who = row_index(l, d)
        return p_all.at[who // 4, q, who % 4]

    for q in range(2):
        p_all[r // 4, q, r % 4] = mine[q * 32:(q + 1) * 32]
    gather_p = Gather(lambda q: p_place(0, 0, 0, q), p_place, ring_x, pair_x, None, send, pa_r)
    gather_p.start()

    def vv_tile(i):
        cols = slice(i * 512, (i + 1) * 512)
        vv[:, cols] = mm(tc[...], vr[...].reshape(512, 1536)[:, cols], 1, 0)

    def z_tile(level, other):
        first = level_of(k, other) * 8 + level_of(zl, level) * 4
        rows = pl.ds(pl.multiple_of(first * 96, 384), 384)
        w[rows, :] = w[rows, :] - mm(z_all[pl.ds(first, 4)].reshape(384, 512), vc[...].reshape(512, 768), 1, 0)

    gather_z.hand_on(0)
    gather_z.relay_pair()
    gather_p.hand_on(0)
    gather_p.relay_pair()
    vv_tile(0)
    gather_z.take_near(0)
    gather_z.hand_on(1)
    gather_z.take_far(0)
    gather_p.hand_on(1)
    gather_z.take_near(1)
    vv_tile(1)
    gather_z.take_far(1)
    vv_tile(2)
    z_tile(0, 0)
    z_tile(1, 0)
    gather_z.take_core(0)
    z_tile(0, 1)
    gather_z.take_core(1)
    z_tile(1, 1)
    gather_p.take_near(0)
    gather_p.take_far(0)
    gather_p.take_near(1)
    gather_p.take_far(1)

    for away, far in halves:
        pl.when(away)(far.wait_send)
    send.finish()
    landed(g_rx, g_s.at[0])
    landed(g_all.at[pl.ds(0, 15)], g_s.at[1])
    landed(s_rx, g_s.at[2])
    landed(s_rx, g_s.at[3])


def last(w, vv, p_all, out, done, sem):
    outs = []
    for i in range(4):
        rows = slice(i * 384, (i + 1) * 384)
        done[rows, :] = w[rows, :] - mm(vv[:, rows], p_all[...].reshape(512, 768), 0, 0)
        copy = pltpu.make_async_copy(done.at[pl.ds(i * 384, 384)], out.at[pl.ds(i * 384, 384)], sem.at[i])
        copy.start()
        outs.append(copy)
    for copy in outs:
        copy.wait()


def body(window, reflectors, factors):
    vt = jnp.swapaxes(reflectors, 1, 2)
    dma = pltpu.SemaphoreType.DMA
    vmem = lambda *s: pltpu.VMEM(s, F32)
    parts = pl.pallas_call(
        kernel,
        out_shape=[jax.ShapeDtypeStruct(q, F32) for q in ((1536, 768), (512, 1536), (2, 2, 4, 32, 768))],
        in_specs=[pl.BlockSpec(memory_space=pltpu.HBM)] * 3,
        out_specs=[pl.BlockSpec(memory_space=pltpu.VMEM)] * 3,
        scratch_shapes=[
            vmem(2, 16, 16, 1536), vmem(2, 16, 16, 768), vmem(2, 256, 256), vmem(512, 512),
            vmem(2, 4, 2, 32, 768), vmem(2, 2, 32, 768), vmem(2, 4, 32, 768), vmem(2, 2, 32, 768),
            vmem(2, 32, 768), vmem(64, 768),
            vmem(2, 384, 512), vmem(2, 384, 512), vmem(2, 4, 96, 512), vmem(2, 96, 512), vmem(2, 2, 96, 512),
            vmem(2, 96, 512), vmem(96, 512), vmem(16, 96, 512),
            vmem(16, 256), vmem(7, 16, 256), vmem(16, 256), vmem(16, 16, 256),
            vmem(2, 64, 256), vmem(15, 8, 256), vmem(8, 256), vmem(2, 64, 256),
            dma((3,)), dma((2,)), dma((2,)), dma((120,)), dma((32,)), dma((16,)), dma((16,)), dma((32,)),
            dma((2, 2)), dma((2, 4)), dma((2,)), dma((2,)), dma((2,)), dma((2, 2)), dma((1,)),
            dma((4,)), dma((4,)),
        ],
        compiler_params=pltpu.CompilerParams(
            has_side_effects=True, collective_id=0, vmem_limit_bytes=40 * 1024 * 1024
        ),
    )(window, vt, factors)
    return pl.pallas_call(
        last,
        out_shape=jax.ShapeDtypeStruct(window.shape, F32),
        in_specs=[pl.BlockSpec(memory_space=pltpu.VMEM)] * 3,
        out_specs=pl.BlockSpec(memory_space=pl.ANY),
        scratch_shapes=[pltpu.VMEM(window.shape, F32), dma((4,))],
        compiler_params=pltpu.CompilerParams(vmem_limit_bytes=14 * 1024 * 1024),
    )(*parts)


def solution(mesh):
    placed = (P("row", "col"), P(None, "row", "col"), P())
    return jax.shard_map(body, mesh=mesh, in_specs=placed, out_specs=P("row", "col"), check_vma=False)
```

```python
import jax
import jax.numpy as jnp
from jax import lax
from jax.experimental import pallas as pl
from jax.experimental.pallas import tpu as pltpu
from jax.sharding import PartitionSpec as P

MESH = pl.DeviceIdType.MESH
F32 = jnp.float32
HIGH = lax.Precision.HIGH


def mm(a, b, ca, cb):
    return lax.dot_general(a, b, (((ca,), (cb,)), ((), ())), precision=HIGH, preferred_element_type=F32)


def remote(src, dst, ssem, rsem, dev):
    return pltpu.make_async_remote_copy(
        src_ref=src, dst_ref=dst, send_sem=ssem, recv_sem=rsem, device_id=dev, device_id_type=MESH
    )


def landed(ref, sem):
    pltpu.make_async_copy(ref, ref, sem).wait()


class Sends:
    def __init__(self, ssem):
        self.ssem, self.started = ssem, []

    def __call__(self, src, dst, rsem, dev):
        copy = remote(src, dst, self.ssem.at[len(self.started)], rsem, dev)
        copy.start()
        self.started.append(copy)

    def finish(self):
        for copy in self.started:
            copy.wait_send()


class Gather:
    def __init__(self, own, place, ring, pair, core, send, rsem):
        self.own, self.place, self.ring, self.pair, self.core = own, place, ring, pair, core
        self.send, self.rsem = send, rsem

    def sem(self, level, d, q, other=0):
        return self.rsem.at[other * 16 + level * 8 + d * 2 + q]

    def start_first(self):
        place = self.place(0, 0, 0, 0)
        self.send(self.own(0), place, self.sem(1, 0, 0), self.pair)
        self.send(self.own(0), place, self.sem(0, 1, 0), self.ring(1))

    def start_second(self):
        place = self.place(0, 0, 0, 1)
        self.send(self.own(1), place, self.sem(1, 0, 1), self.pair)
        self.send(self.own(1), place, self.sem(0, 3, 1), self.ring(3))
        self.send(self.own(1), place, self.sem(0, 1, 1), self.ring(1))
        self.send(self.own(0), self.place(0, 0, 0, 0), self.sem(0, 3, 0), self.ring(3))
        if self.core is not None:
            for q in (0, 1):
                self.send(self.own(q), self.place(0, 0, 0, q), self.sem(0, 0, q, 1), self.core)

    def wait(self, level, d, q, other=0):
        landed(self.place(level, d, other, q), self.sem(level, d, q, other))

    def to_core(self, level, d, q):
        if self.core is not None:
            place = self.place(level, d, 0, q)
            self.send(place, place, self.sem(level, d, q, 1), self.core)

    def hand_on(self, level, q):
        d = 1 if q == 0 else 3
        self.wait(level, d, q)
        place = self.place(level, d, 0, q)
        self.send(place, place, self.sem(level, 2, q), self.ring(d))
        self.to_core(level, d, q)

    def relay_pair(self):
        first, second = self.place(1, 0, 0, 0), self.place(1, 0, 0, 1)
        self.wait(1, 0, 0)
        self.send(first, first, self.sem(1, 1, 0), self.ring(1))
        self.wait(1, 0, 1)
        self.send(second, second, self.sem(1, 3, 1), self.ring(3))
        self.send(second, second, self.sem(1, 1, 1), self.ring(1))
        self.send(first, first, self.sem(1, 3, 0), self.ring(3))
        self.to_core(1, 0, 0)
        self.to_core(1, 0, 1)

    def take_near(self, level, q):
        d = 3 if q == 0 else 1
        self.wait(level, d, q)
        self.to_core(level, d, q)

    def take_far(self, level, q):
        self.wait(level, 2, q)
        self.to_core(level, 2, q)

    def take_core(self, level, q):
        for d in (0, 1, 3, 2):
            self.wait(level, d, q, 1)


def kernel(
    w_hbm, v_hbm, t_hbm, w, vv, p_all,
    vr, vc, tf, tc,
    p, p_far, p_rx, p_acc, p_pair, p_own,
    y_send, y_core, y_own, y_far, y_rx, y_acc, y_pair, z_all,
    g_part, g_rx, g_own, g_all, s_part, s_rx, s_own, s_all,
    load_sem, zero_s, zero_r, all_s, vr_r, vc_r, pa_r, za_r,
    pf_r, p_r, pz_r, yc_r, yf_r, y_r, yz_r, g_s, g_r,
):
    r = lax.axis_index("row")
    c = lax.axis_index("col")
    x, zh = r // 2, r % 2
    zl, y, k = c // 8, (c // 2) % 4, c % 2

    def dev(x_, zh_, zl_, y_, k_):
        return (x_ * 2 + zh_, (zl_ * 4 + y_) * 2 + k_)

    def ring_x(d):
        return dev((x + d) % 4, zh, zl, y, k)

    def ring_y(d):
        return dev(x, zh, zl, (y + d) % 4, k)

    pair_x = dev(x, 1 - zh, zl, y, k)
    pair_y = dev(x, zh, 1 - zl, y, k)
    core = dev(x, zh, zl, y, 1 - k)

    def level_of(z, level):
        return z if level == 0 else 1 - z

    def col_index(level, d, other):
        return (level_of(zl, level) * 4 + (y + 4 - d) % 4) * 2 + level_of(k, other)

    def row_index(level, d):
        return ((x + 4 - d) % 4) * 2 + level_of(zh, level)

    def vc_pair(level, d):
        other_x = (x + 4 - d) % 4
        return (level_of(zh, level) + c // 2) % 2 * 4 + (other_x + 4 - c // 4) % 4

    load_w = pltpu.make_async_copy(w_hbm, w, load_sem.at[1])
    load_w.start()
    own_v = pltpu.make_async_copy(v_hbm, vr.at[:, c], load_sem.at[0])
    own_v.start()
    load_t = pltpu.make_async_copy(t_hbm, tf, load_sem.at[2])
    load_t.start()

    target = (x + y) % 4 * 2 + (zh + zl) % 2
    share = vc_pair(0, 0)
    barrier = pltpu.get_barrier_semaphore()

    def greet(device):
        pl.semaphore_signal(barrier, inc=1, device_id=device, device_id_type=MESH)

    for h in range(2):
        apart = jnp.logical_not(jnp.logical_and(target == r, 2 * r + h == c))
        pl.when(apart)(lambda h=h: greet((target, 2 * r + h)))
        apart = jnp.logical_not(jnp.logical_and(c // 2 == r, 2 * share + h == c))
        pl.when(apart)(lambda h=h: greet((c // 2, 2 * share + h)))
    for device in (ring_y(1), ring_y(3), pair_y, core):
        greet(device)
    for i in range(1, 8):
        greet(((r + i) % 8, c))
    home = jnp.logical_and(r == 0, c // 2 == 0)
    pl.semaphore_wait(barrier, 15 - 2 * home.astype(jnp.int32))

    halves = []
    for q in range(2):
        for h in range(2):
            src = v_hbm.at[q, :, pl.ds(h * 768, 768)]
            at_home = jnp.logical_and(target == r, 2 * r + h == c)
            away = jnp.logical_not(at_home)
            local = pltpu.make_async_copy(src, vc.at[q, c], zero_r.at[k, q])
            far = remote(src, vc.at[q, c], zero_s.at[h, q], zero_r.at[k, q], (target, 2 * r + h))
            pl.when(at_home)(local.start)
            pl.when(away)(far.start)
            halves.append((away, far))
    send = Sends(all_s)
    vr_place = lambda panel: lambda l, d, o, q: vr.at[panel, col_index(l, d, o), pl.ds(q * 8, 8)]
    vr0, vr1 = (
        Gather(
            lambda q, i=i: v_hbm.at[i, pl.ds(q * 8, 8)], vr_place(i), ring_y, pair_y, core, send, vr_r.at[i]
        )
        for i in range(2)
    )
    for gather in (vr0, vr1):
        gather.start_first()
        gather.start_second()

    def vc_gather(panel):
        place = lambda l, d, o, q: vc.at[panel, 2 * vc_pair(l, d) + q]
        return Gather(lambda q: place(0, 0, 0, q), place, ring_x, pair_x, None, send, vc_r.at[panel])

    vc0, vc1 = vc_gather(0), vc_gather(1)

    def vc_start(panel):
        gather = vc1 if panel else vc0
        for q in range(2):
            landed(vc.at[panel, 2 * share + q], zero_r.at[q, panel])
            (gather.start_second if q else gather.start_first)()

    def both(step, *where):
        for q in range(2):
            step(*where, q)

    vc_start(0)
    both(vr0.hand_on, 0)
    vr0.relay_pair()
    vc_start(1)
    both(vr1.hand_on, 0)
    vr1.relay_pair()
    both(vc0.hand_on, 0)
    both(vr0.take_near, 0)
    both(vr0.hand_on, 1)
    vc0.relay_pair()
    both(vr0.take_far, 0)
    both(vr1.take_near, 0)
    both(vc1.hand_on, 0)
    both(vr1.hand_on, 1)
    vc1.relay_pair()
    both(vr0.take_near, 1)
    both(vr0.take_far, 1)
    both(vr1.take_far, 0)
    own_v.wait()
    load_w.wait()
    load_t.wait()

    def p_product(m, n):
        cols = slice(n * 256, n * 256 + 256)
        p[m, :, :, :, cols] = mm(vr[m].reshape(256, 1536), w[:, cols], 1, 0).reshape(4, 2, 32, 256)

    def p_start(m):
        right, left, far = (x + 1) % 4, (x + 3) % 4, (x + 2) % 4
        send(p.at[m, far, 0], p_far.at[m, 0], pf_r.at[m, 0], ring_x(1))
        send(p.at[m, far, 1], p_far.at[m, 1], pf_r.at[m, 1], ring_x(3))
        send(p.at[m, right, 1], p_rx.at[m, 0], p_r.at[m, 0], ring_x(1))
        send(p.at[m, left, 0], p_rx.at[m, 1], p_r.at[m, 1], ring_x(3))

    def p_hand_on(m):
        right, left = (x + 1) % 4, (x + 3) % 4
        landed(p_far.at[m, 0], pf_r.at[m, 0])
        p[m, right, 0] = p[m, right, 0] + p_far[m, 0]
        send(p.at[m, right, 0], p_rx.at[m, 2], p_r.at[m, 2], ring_x(1))
        landed(p_far.at[m, 1], pf_r.at[m, 1])
        p[m, left, 1] = p[m, left, 1] + p_far[m, 1]
        send(p.at[m, left, 1], p_rx.at[m, 3], p_r.at[m, 3], ring_x(3))

    def p_sum(m):
        for i in range(4):
            landed(p_rx.at[m, i], p_r.at[m, i])
        p_acc[m, 0] = p[m, x, 0] + (p_rx[m, 1] + p_rx[m, 2])
        p_acc[m, 1] = p[m, x, 1] + (p_rx[m, 0] + p_rx[m, 3])
        send(p_acc.at[m, 1 - zh], p_pair.at[m], pz_r.at[m], pair_x)

    def p_take(m):
        landed(p_pair.at[m], pz_r.at[m])
        p_own[m * 32:(m + 1) * 32, :] = p_acc[m, zh] + p_pair[m]

    def y_tile(panel, row):
        rows = pl.ds(pl.multiple_of(row, 384), 384)
        return mm(w[rows, :], vc[panel].reshape(256, 768), 1, 1)

    def y_other(i, t):
        y_send[i, t] = y_tile(i, (1 - k) * 768 + t * 384)
        send(y_send.at[i, t], y_core.at[i, t], yc_r.at[i, t], core)

    def y_mine(i, t):
        part = y_tile(i, k * 768 + t * 384)
        landed(y_core.at[i, t], yc_r.at[i, t])
        y_own[i, t] = (part + y_core[i, t]).reshape(4, 2, 48, 256)
        send(y_own.at[i, t, (y + 2) % 4], y_far.at[i, t], yf_r.at[i, t], ring_y(3 if t else 1))

    def y_plain(i):
        for t, behind in ((1, 1), (0, 3)):
            send(y_own.at[i, t, (y + behind) % 4], y_rx.at[i, t, 1], y_r.at[i, t, 1], ring_y(behind))

    def y_hand_on(i, t):
        ahead = 1 if t == 0 else 3
        to = (y + ahead) % 4
        landed(y_far.at[i, t], yf_r.at[i, t])
        y_own[i, t, to] = y_own[i, t, to] + y_far[i, t]
        send(y_own.at[i, t, to], y_rx.at[i, t, 0], y_r.at[i, t, 0], ring_y(ahead))

    def y_sum(i, t):
        landed(y_rx.at[i, t, 0], y_r.at[i, t, 0])
        landed(y_rx.at[i, t, 1], y_r.at[i, t, 1])
        y_acc[i, t] = y_own[i, t, y] + (y_rx[i, t, 0] + y_rx[i, t, 1])
        send(y_acc.at[i, t, 1 - zl], y_pair.at[i, t], yz_r.at[i, t], pair_y)

    def vv_tile(i):
        cols = slice(i * 512, (i + 1) * 512)
        vv[:, cols] = mm(tc[...], vr[...].reshape(512, 1536)[:, cols], 1, 0)

    def g_product():
        g_part[...] = mm(vr[0, c], vr[1].reshape(256, 1536), 1, 1)

        def each(i, _):
            remote(g_part, g_rx.at[i], g_s.at[0], g_r.at[0], ((r + 1 + i) % 8, c)).start()
            return 0

        lax.fori_loop(0, 7, each, 0)

    def g_sum():
        landed(g_rx, g_r.at[0])
        g_own[...] = (g_part[...] + g_rx[0] + g_rx[1] + g_rx[2]) + (g_rx[3] + g_rx[4] + g_rx[5] + g_rx[6])
        g_all[c] = g_own[...]

        def each(i, _):
            remote(g_own, g_all.at[c], g_s.at[1], g_r.at[1], (r, (c + 1 + i) % 16)).start()
            return 0

        lax.fori_loop(0, 15, each, 0)

    def join_factors():
        landed(g_all.at[pl.ds(0, 15)], g_r.at[1])
        tc[0:256, 0:256] = tf[0]
        tc[256:512, 256:512] = tf[1]
        tc[256:512, 0:256] = jnp.zeros((256, 256), F32)
        tc[0:256, 256:512] = -mm(mm(tf[0], g_all[...].reshape(256, 256), 1, 0), tf[1], 1, 0)

    def chunk(ref, who):
        return ref.at[who % 2, pl.ds(pl.multiple_of(who // 2 * 8, 8), 8)]

    def s_product():
        part = mm(p_own[...], vc[...].reshape(512, 768), 1, 1)
        s_part[0] = part[:, :256]
        s_part[1] = part[:, 256:]

        def each(i, _):
            to = (c + 1 + i) % 16
            remote(chunk(s_part, to), s_rx.at[i], g_s.at[2], g_r.at[2], (r, to)).start()
            return 0

        lax.fori_loop(0, 15, each, 0)

    def s_sum():
        landed(s_rx, g_r.at[2])
        total = s_part[k, pl.ds(pl.multiple_of(c // 2 * 8, 8), 8)]
        for i in range(15):
            total = total + s_rx[i]
        s_own[...] = total
        s_all[k, pl.ds(pl.multiple_of(c // 2 * 8, 8), 8)] = total

        def each(i, _):
            remote(s_own, chunk(s_all, c), g_s.at[3], g_r.at[3], (r, (c + 1 + i) % 16)).start()
            return 0

        lax.fori_loop(0, 15, each, 0)

    def z_place(level, d, other, q):
        return z_all.at[level_of(k, other), q, (y + 4 - d) % 4, level_of(zl, level)]

    gather_z = Gather(lambda q: z_place(0, 0, 0, q), z_place, ring_y, pair_y, core, send, za_r)

    def z_start(t):
        for i in range(2):
            landed(y_pair.at[i, t], yz_r.at[i, t])
        rows = jnp.concatenate([y_acc[i, t, zl] + y_pair[i, t] for i in range(2)], axis=1)
        z_all[k, t, y, zl] = mm(rows, tc[...], 1, 0)
        (gather_z.start_second if t else gather_z.start_first)()

    def z_tile(other, t):
        half = level_of(k, other)
        rows = pl.ds(pl.multiple_of(half * 768 + t * 384, 384), 384)
        w[rows, :] = w[rows, :] - mm(z_all[half, t].reshape(384, 512), vc[...].reshape(512, 768), 1, 0)

    def p_place(level, d, other, q):
        return p_all.at[q, row_index(level, d)]

    gather_p = Gather(lambda q: p_place(0, 0, 0, q), p_place, ring_x, pair_x, None, send, pa_r)

    def p_correct():
        landed(s_rx, g_r.at[3])
        s_rows = jnp.concatenate([s_all[0], s_all[1]], axis=1)
        mine = p_own[...] - mm(mm(s_rows, tc[...], 1, 0), vc[...].reshape(512, 768), 1, 0)
        for q in range(2):
            p_all[q, r] = mine[q * 32:(q + 1) * 32]
        gather_p.start_first()
        gather_p.start_second()

    both(vr0.take_core, 0)
    both(vr0.take_core, 1)
    p_product(0, 0)
    both(vr1.take_near, 1)
    both(vr1.take_far, 1)
    both(vc0.hand_on, 1)
    p_product(0, 1)
    p_product(0, 2)
    p_start(0)
    both(vc1.hand_on, 1)
    for level in range(2):
        both(vc0.take_near, level)
        both(vc0.take_far, level)
    y_other(0, 0)
    y_other(0, 1)
    both(vr1.take_core, 0)
    both(vr1.take_core, 1)
    g_product()
    for n in range(3):
        p_product(1, n)
    p_start(1)
    y_mine(0, 0)
    y_mine(0, 1)
    y_plain(0)
    p_hand_on(0)
    g_sum()
    for level in range(2):
        both(vc1.take_near, level)
        both(vc1.take_far, level)
    y_other(1, 0)
    y_other(1, 1)
    p_hand_on(1)
    y_hand_on(0, 0)
    y_hand_on(0, 1)
    y_mine(1, 0)
    y_mine(1, 1)
    y_plain(1)
    p_sum(0)
    join_factors()
    p_sum(1)
    y_hand_on(1, 0)
    y_hand_on(1, 1)
    y_sum(0, 0)
    y_sum(0, 1)
    p_take(0)
    p_take(1)
    s_product()
    y_sum(1, 0)
    y_sum(1, 1)
    s_sum()
    z_start(0)
    z_start(1)
    p_correct()
    both(gather_z.hand_on, 0)
    gather_z.relay_pair()
    vv_tile(0)
    both(gather_p.hand_on, 0)
    gather_p.relay_pair()
    vv_tile(1)
    both(gather_z.take_near, 0)
    both(gather_z.hand_on, 1)
    vv_tile(2)
    both(gather_z.take_far, 0)
    both(gather_p.hand_on, 1)
    both(gather_z.take_near, 1)
    both(gather_z.take_far, 1)
    z_tile(0, 0)
    z_tile(0, 1)
    for q in range(2):
        for level in range(2):
            gather_z.take_core(level, q)
        z_tile(1, q)
    for level in range(2):
        both(gather_p.take_near, level)
        both(gather_p.take_far, level)

    for away, far in halves:
        pl.when(away)(far.wait_send)
    send.finish()
    landed(g_rx, g_s.at[0])
    landed(g_all.at[pl.ds(0, 15)], g_s.at[1])
    landed(s_rx, g_s.at[2])
    landed(s_rx, g_s.at[3])


def last(w, vv, p_all, out, done, sem):
    outs = []
    for i in range(4):
        rows = slice(i * 384, (i + 1) * 384)
        done[rows, :] = w[rows, :] - mm(vv[:, rows], p_all[...].reshape(512, 768), 0, 0)
        copy = pltpu.make_async_copy(done.at[pl.ds(i * 384, 384)], out.at[pl.ds(i * 384, 384)], sem.at[i])
        copy.start()
        outs.append(copy)
    for copy in outs:
        copy.wait()


def body(window, reflectors, factors):
    vt = jnp.swapaxes(reflectors, 1, 2)
    dma = pltpu.SemaphoreType.DMA
    vmem = lambda *s: pltpu.VMEM(s, F32)
    parts = pl.pallas_call(
        kernel,
        out_shape=[jax.ShapeDtypeStruct(q, F32) for q in ((1536, 768), (512, 1536), (2, 8, 32, 768))],
        in_specs=[pl.BlockSpec(memory_space=pltpu.HBM)] * 3,
        out_specs=[pl.BlockSpec(memory_space=pltpu.VMEM)] * 3,
        scratch_shapes=[
            vmem(2, 16, 16, 1536), vmem(2, 16, 16, 768), vmem(2, 256, 256), vmem(512, 512),
            vmem(2, 4, 2, 32, 768), vmem(2, 2, 32, 768), vmem(2, 4, 32, 768), vmem(2, 2, 32, 768),
            vmem(2, 32, 768), vmem(64, 768),
            vmem(2, 2, 384, 256), vmem(2, 2, 384, 256), vmem(2, 2, 4, 2, 48, 256), vmem(2, 2, 2, 48, 256),
            vmem(2, 2, 2, 2, 48, 256), vmem(2, 2, 2, 48, 256), vmem(2, 2, 48, 256), vmem(2, 2, 4, 2, 48, 512),
            vmem(16, 256), vmem(7, 16, 256), vmem(16, 256), vmem(16, 16, 256),
            vmem(2, 64, 256), vmem(15, 8, 256), vmem(8, 256), vmem(2, 64, 256),
            dma((3,)), dma((2, 2)), dma((2, 2)), dma((180,)), dma((2, 32)), dma((2, 16)), dma((16,)), dma((32,)),
            dma((2, 2)), dma((2, 4)), dma((2,)), dma((2, 2)), dma((2, 2)), dma((2, 2, 2)), dma((2, 2)),
            dma((4,)), dma((4,)),
        ],
        compiler_params=pltpu.CompilerParams(
            has_side_effects=True, collective_id=0, vmem_limit_bytes=40 * 1024 * 1024
        ),
    )(*(pltpu.with_memory_space_constraint(a, pltpu.HBM) for a in (window, vt, factors)))
    return pl.pallas_call(
        last,
        out_shape=jax.ShapeDtypeStruct(window.shape, F32),
        in_specs=[pl.BlockSpec(memory_space=pltpu.VMEM)] * 3,
        out_specs=pl.BlockSpec(memory_space=pl.ANY),
        scratch_shapes=[pltpu.VMEM(window.shape, F32), dma((4,))],
        compiler_params=pltpu.CompilerParams(vmem_limit_bytes=14 * 1024 * 1024),
    )(*parts)


def solution(mesh):
    placed = (P("row", "col"), P(None, "row", "col"), P())
    return jax.shard_map(body, mesh=mesh, in_specs=placed, out_specs=P("row", "col"), check_vma=False)
```

```python
import jax
import jax.numpy as jnp
from jax import lax
from jax.experimental import pallas as pl
from jax.experimental.pallas import tpu as pltpu
from jax.sharding import PartitionSpec as P

MESH = pl.DeviceIdType.MESH
F32 = jnp.float32
HIGH = lax.Precision.HIGH


def mm(a, b, ca, cb):
    return lax.dot_general(a, b, (((ca,), (cb,)), ((), ())), precision=HIGH, preferred_element_type=F32)


def remote(src, dst, ssem, rsem, dev):
    return pltpu.make_async_remote_copy(
        src_ref=src, dst_ref=dst, send_sem=ssem, recv_sem=rsem, device_id=dev, device_id_type=MESH
    )


def landed(ref, sem):
    pltpu.make_async_copy(ref, ref, sem).wait()


class Sends:
    def __init__(self, ssem):
        self.ssem, self.started = ssem, []

    def __call__(self, src, dst, rsem, dev):
        copy = remote(src, dst, self.ssem.at[len(self.started)], rsem, dev)
        copy.start()
        self.started.append(copy)

    def finish(self):
        for copy in self.started:
            copy.wait_send()


class Gather:
    def __init__(self, own, place, ring, pair, core, send, rsem):
        self.own, self.place, self.ring, self.pair, self.core = own, place, ring, pair, core
        self.send, self.rsem = send, rsem

    def sem(self, level, d, q, other=0):
        return self.rsem.at[other * 16 + level * 8 + d * 2 + q]

    def start_first(self):
        place = self.place(0, 0, 0, 0)
        self.send(self.own(0), place, self.sem(1, 0, 0), self.pair)
        self.send(self.own(0), place, self.sem(0, 1, 0), self.ring(1))

    def start_second(self):
        place = self.place(0, 0, 0, 1)
        self.send(self.own(1), place, self.sem(1, 0, 1), self.pair)
        self.send(self.own(1), place, self.sem(0, 3, 1), self.ring(3))
        self.send(self.own(1), place, self.sem(0, 1, 1), self.ring(1))
        self.send(self.own(0), self.place(0, 0, 0, 0), self.sem(0, 3, 0), self.ring(3))
        if self.core is not None:
            for q in (0, 1):
                self.send(self.own(q), self.place(0, 0, 0, q), self.sem(0, 0, q, 1), self.core)

    def wait(self, level, d, q, other=0):
        landed(self.place(level, d, other, q), self.sem(level, d, q, other))

    def to_core(self, level, d, q):
        if self.core is not None:
            place = self.place(level, d, 0, q)
            self.send(place, place, self.sem(level, d, q, 1), self.core)

    def hand_on(self, level, q):
        d = 1 if q == 0 else 3
        self.wait(level, d, q)
        place = self.place(level, d, 0, q)
        self.send(place, place, self.sem(level, 2, q), self.ring(d))
        self.to_core(level, d, q)

    def relay_pair(self):
        first, second = self.place(1, 0, 0, 0), self.place(1, 0, 0, 1)
        self.wait(1, 0, 0)
        self.send(first, first, self.sem(1, 1, 0), self.ring(1))
        self.wait(1, 0, 1)
        self.send(second, second, self.sem(1, 3, 1), self.ring(3))
        self.send(second, second, self.sem(1, 1, 1), self.ring(1))
        self.send(first, first, self.sem(1, 3, 0), self.ring(3))
        self.to_core(1, 0, 0)
        self.to_core(1, 0, 1)

    def take_near(self, level, q):
        d = 3 if q == 0 else 1
        self.wait(level, d, q)
        self.to_core(level, d, q)

    def take_far(self, level, q):
        self.wait(level, 2, q)
        self.to_core(level, 2, q)

    def take_core(self, level, q):
        for d in (0, 1, 3, 2):
            self.wait(level, d, q, 1)


def kernel(
    w_hbm, v_hbm, t_hbm, w, vv, p_all,
    vr, vc, tf, tc,
    p, p_far, p_rx, p_acc, p_pair, p_own,
    y_send, y_core, y_own, y_far, y_rx, y_acc, y_pair, z_all,
    g_part, g_rx, g_own, g_all, s_part, s_rx, s_own, s_all,
    load_sem, zero_s, zero_r, all_s, vr_r, vc_r, pa_r, za_r,
    pf_r, p_r, pz_r, yc_r, yf_r, y_r, yz_r, g_s, g_r,
):
    r = lax.axis_index("row")
    c = lax.axis_index("col")
    x, zh = r // 2, r % 2
    zl, y, k = c // 8, (c // 2) % 4, c % 2

    def dev(x_, zh_, zl_, y_, k_):
        return (x_ * 2 + zh_, (zl_ * 4 + y_) * 2 + k_)

    def ring_x(d):
        return dev((x + d) % 4, zh, zl, y, k)

    def ring_y(d):
        return dev(x, zh, zl, (y + d) % 4, k)

    pair_x = dev(x, 1 - zh, zl, y, k)
    pair_y = dev(x, zh, 1 - zl, y, k)
    core = dev(x, zh, zl, y, 1 - k)

    def level_of(z, level):
        return z if level == 0 else 1 - z

    def col_index(level, d, other):
        return (level_of(zl, level) * 4 + (y + 4 - d) % 4) * 2 + level_of(k, other)

    def row_index(level, d):
        return ((x + 4 - d) % 4) * 2 + level_of(zh, level)

    def vc_pair(level, d):
        other_x = (x + 4 - d) % 4
        return (level_of(zh, level) + c // 2) % 2 * 4 + (other_x + 4 - c // 4) % 4

    load_w = pltpu.make_async_copy(w_hbm, w, load_sem.at[1])
    load_w.start()
    own_v = pltpu.make_async_copy(v_hbm, vr.at[:, c], load_sem.at[0])
    own_v.start()
    load_t = pltpu.make_async_copy(t_hbm, tf, load_sem.at[2])
    load_t.start()

    target = (x + y) % 4 * 2 + (zh + zl) % 2
    share = vc_pair(0, 0)
    barrier = pltpu.get_barrier_semaphore()

    def greet(device):
        pl.semaphore_signal(barrier, inc=1, device_id=device, device_id_type=MESH)

    for h in range(2):
        apart = jnp.logical_not(jnp.logical_and(target == r, 2 * r + h == c))
        pl.when(apart)(lambda h=h: greet((target, 2 * r + h)))
        apart = jnp.logical_not(jnp.logical_and(c // 2 == r, 2 * share + h == c))
        pl.when(apart)(lambda h=h: greet((c // 2, 2 * share + h)))
    for device in (ring_y(1), ring_y(3), pair_y, core):
        greet(device)
    for i in range(1, 8):
        greet(((r + i) % 8, c))
    home = jnp.logical_and(r == 0, c // 2 == 0)
    pl.semaphore_wait(barrier, 15 - 2 * home.astype(jnp.int32))

    halves = []
    for q in range(2):
        for h in range(2):
            src = v_hbm.at[q, :, pl.ds(h * 768, 768)]
            at_home = jnp.logical_and(target == r, 2 * r + h == c)
            away = jnp.logical_not(at_home)
            local = pltpu.make_async_copy(src, vc.at[q, c], zero_r.at[k, q])
            far = remote(src, vc.at[q, c], zero_s.at[h, q], zero_r.at[k, q], (target, 2 * r + h))
            pl.when(at_home)(local.start)
            pl.when(away)(far.start)
            halves.append((away, far))
    send = Sends(all_s)
    vr_place = lambda panel: lambda l, d, o, q: vr.at[panel, col_index(l, d, o), pl.ds(q * 8, 8)]
    vr0, vr1 = (
        Gather(
            lambda q, i=i: v_hbm.at[i, pl.ds(q * 8, 8)], vr_place(i), ring_y, pair_y, core, send, vr_r.at[i]
        )
        for i in range(2)
    )
    for gather in (vr0, vr1):
        gather.start_first()
        gather.start_second()

    def vc_gather(panel):
        place = lambda l, d, o, q: vc.at[panel, 2 * vc_pair(l, d) + q]
        return Gather(lambda q: place(0, 0, 0, q), place, ring_x, pair_x, None, send, vc_r.at[panel])

    vc0, vc1 = vc_gather(0), vc_gather(1)

    def vc_start(panel):
        gather = vc1 if panel else vc0
        for q in range(2):
            landed(vc.at[panel, 2 * share + q], zero_r.at[q, panel])
            (gather.start_second if q else gather.start_first)()

    def both(step, *where):
        for q in range(2):
            step(*where, q)

    vc_start(0)
    both(vr0.hand_on, 0)
    vr0.relay_pair()
    vc_start(1)
    both(vr1.hand_on, 0)
    vr1.relay_pair()
    both(vc0.hand_on, 0)
    both(vr0.take_near, 0)
    both(vr0.hand_on, 1)
    vc0.relay_pair()
    both(vr0.take_far, 0)
    both(vr1.take_near, 0)
    both(vc1.hand_on, 0)
    both(vr1.hand_on, 1)
    vc1.relay_pair()
    both(vr0.take_near, 1)
    both(vr0.take_far, 1)
    both(vr1.take_far, 0)
    own_v.wait()
    load_w.wait()
    load_t.wait()

    def p_product(m, n):
        cols = slice(n * 256, n * 256 + 256)
        p[m, :, :, :, cols] = mm(vr[m].reshape(256, 1536), w[:, cols], 1, 0).reshape(4, 2, 32, 256)

    def p_start(m):
        right, left, far = (x + 1) % 4, (x + 3) % 4, (x + 2) % 4
        send(p.at[m, far, 0], p_far.at[m, 0], pf_r.at[m, 0], ring_x(1))
        send(p.at[m, far, 1], p_far.at[m, 1], pf_r.at[m, 1], ring_x(3))
        send(p.at[m, right, 1], p_rx.at[m, 0], p_r.at[m, 0], ring_x(1))
        send(p.at[m, left, 0], p_rx.at[m, 1], p_r.at[m, 1], ring_x(3))

    def p_hand_on(m):
        right, left = (x + 1) % 4, (x + 3) % 4
        landed(p_far.at[m, 0], pf_r.at[m, 0])
        p[m, right, 0] = p[m, right, 0] + p_far[m, 0]
        send(p.at[m, right, 0], p_rx.at[m, 2], p_r.at[m, 2], ring_x(1))
        landed(p_far.at[m, 1], pf_r.at[m, 1])
        p[m, left, 1] = p[m, left, 1] + p_far[m, 1]
        send(p.at[m, left, 1], p_rx.at[m, 3], p_r.at[m, 3], ring_x(3))

    def p_sum(m):
        for i in range(4):
            landed(p_rx.at[m, i], p_r.at[m, i])
        p_acc[m, 0] = p[m, x, 0] + (p_rx[m, 1] + p_rx[m, 2])
        p_acc[m, 1] = p[m, x, 1] + (p_rx[m, 0] + p_rx[m, 3])
        send(p_acc.at[m, 1 - zh], p_pair.at[m], pz_r.at[m], pair_x)

    def p_take(m):
        landed(p_pair.at[m], pz_r.at[m])
        p_own[m * 32:(m + 1) * 32, :] = p_acc[m, zh] + p_pair[m]

    def y_tile(panel, row):
        rows = pl.ds(pl.multiple_of(row, 384), 384)
        return mm(w[rows, :], vc[panel].reshape(256, 768), 1, 1)

    def y_other(i, t):
        y_send[i, t] = y_tile(i, (1 - k) * 768 + t * 384)
        send(y_send.at[i, t], y_core.at[i, t], yc_r.at[i, t], core)

    def y_mine(i, t):
        part = y_tile(i, k * 768 + t * 384)
        landed(y_core.at[i, t], yc_r.at[i, t])
        y_own[i, t] = (part + y_core[i, t]).reshape(4, 2, 48, 256)
        send(y_own.at[i, t, (y + 2) % 4], y_far.at[i, t], yf_r.at[i, t], ring_y(3 if t else 1))

    def y_plain(i):
        for t, behind in ((1, 1), (0, 3)):
            send(y_own.at[i, t, (y + behind) % 4], y_rx.at[i, t, 1], y_r.at[i, t, 1], ring_y(behind))

    def y_hand_on(i, t):
        ahead = 1 if t == 0 else 3
        to = (y + ahead) % 4
        landed(y_far.at[i, t], yf_r.at[i, t])
        y_own[i, t, to] = y_own[i, t, to] + y_far[i, t]
        send(y_own.at[i, t, to], y_rx.at[i, t, 0], y_r.at[i, t, 0], ring_y(ahead))

    def y_sum(i, t):
        landed(y_rx.at[i, t, 0], y_r.at[i, t, 0])
        landed(y_rx.at[i, t, 1], y_r.at[i, t, 1])
        y_acc[i, t] = y_own[i, t, y] + (y_rx[i, t, 0] + y_rx[i, t, 1])
        send(y_acc.at[i, t, 1 - zl], y_pair.at[i, t], yz_r.at[i, t], pair_y)

    def vv_tile(i):
        cols = slice(i * 512, (i + 1) * 512)
        vv[:, cols] = mm(tc[...], vr[...].reshape(512, 1536)[:, cols], 1, 0)

    def g_product():
        g_part[...] = mm(vr[0, c], vr[1].reshape(256, 1536), 1, 1)

        def each(i, _):
            remote(g_part, g_rx.at[i], g_s.at[0], g_r.at[0], ((r + 1 + i) % 8, c)).start()
            return 0

        lax.fori_loop(0, 7, each, 0)

    def g_sum():
        landed(g_rx, g_r.at[0])
        g_own[...] = (g_part[...] + g_rx[0] + g_rx[1] + g_rx[2]) + (g_rx[3] + g_rx[4] + g_rx[5] + g_rx[6])
        g_all[c] = g_own[...]

        def each(i, _):
            remote(g_own, g_all.at[c], g_s.at[1], g_r.at[1], (r, (c + 1 + i) % 16)).start()
            return 0

        lax.fori_loop(0, 15, each, 0)

    def join_factors():
        landed(g_all.at[pl.ds(0, 15)], g_r.at[1])
        tc[0:256, 0:256] = tf[0]
        tc[256:512, 256:512] = tf[1]
        tc[256:512, 0:256] = jnp.zeros((256, 256), F32)
        tc[0:256, 256:512] = -mm(mm(tf[0], g_all[...].reshape(256, 256), 1, 0), tf[1], 1, 0)

    def chunk(ref, who):
        return ref.at[who % 2, pl.ds(pl.multiple_of(who // 2 * 8, 8), 8)]

    def s_product():
        part = mm(p_own[...], vc[...].reshape(512, 768), 1, 1)
        s_part[0] = part[:, :256]
        s_part[1] = part[:, 256:]

        def each(i, _):
            to = (c + 1 + i) % 16
            remote(chunk(s_part, to), s_rx.at[i], g_s.at[2], g_r.at[2], (r, to)).start()
            return 0

        lax.fori_loop(0, 15, each, 0)

    def s_sum():
        landed(s_rx, g_r.at[2])
        total = s_part[k, pl.ds(pl.multiple_of(c // 2 * 8, 8), 8)]
        for i in range(15):
            total = total + s_rx[i]
        s_own[...] = total
        s_all[k, pl.ds(pl.multiple_of(c // 2 * 8, 8), 8)] = total

        def each(i, _):
            remote(s_own, chunk(s_all, c), g_s.at[3], g_r.at[3], (r, (c + 1 + i) % 16)).start()
            return 0

        lax.fori_loop(0, 15, each, 0)

    def z_place(level, d, other, q):
        return z_all.at[level_of(k, other), q, (y + 4 - d) % 4, level_of(zl, level)]

    gather_z = Gather(lambda q: z_place(0, 0, 0, q), z_place, ring_y, pair_y, core, send, za_r)

    def z_start(t):
        for i in range(2):
            landed(y_pair.at[i, t], yz_r.at[i, t])
        rows = jnp.concatenate([y_acc[i, t, zl] + y_pair[i, t] for i in range(2)], axis=1)
        z_all[k, t, y, zl] = mm(rows, tc[...], 1, 0)
        (gather_z.start_second if t else gather_z.start_first)()

    def z_tile(other, t):
        half = level_of(k, other)
        rows = pl.ds(pl.multiple_of(half * 768 + t * 384, 384), 384)
        w[rows, :] = w[rows, :] - mm(z_all[half, t].reshape(384, 512), vc[...].reshape(512, 768), 1, 0)

    def p_place(level, d, other, q):
        return p_all.at[q, row_index(level, d)]

    gather_p = Gather(lambda q: p_place(0, 0, 0, q), p_place, ring_x, pair_x, None, send, pa_r)

    def p_correct():
        landed(s_rx, g_r.at[3])
        s_rows = jnp.concatenate([s_all[0], s_all[1]], axis=1)
        mine = p_own[...] - mm(mm(s_rows, tc[...], 1, 0), vc[...].reshape(512, 768), 1, 0)
        for q in range(2):
            p_all[q, r] = mine[q * 32:(q + 1) * 32]
        gather_p.start_first()
        gather_p.start_second()

    both(vr0.take_core, 0)
    both(vr0.take_core, 1)
    p_product(0, 0)
    both(vr1.take_near, 1)
    both(vr1.take_far, 1)
    both(vc0.hand_on, 1)
    p_product(0, 1)
    p_product(0, 2)
    p_start(0)
    both(vc1.hand_on, 1)
    for level in range(2):
        both(vc0.take_near, level)
        both(vc0.take_far, level)
    y_other(0, 0)
    y_other(0, 1)
    both(vr1.take_core, 0)
    both(vr1.take_core, 1)
    g_product()
    for n in range(3):
        p_product(1, n)
    p_start(1)
    y_mine(0, 0)
    y_mine(0, 1)
    y_plain(0)
    p_hand_on(0)
    g_sum()
    for level in range(2):
        both(vc1.take_near, level)
        both(vc1.take_far, level)
    y_other(1, 0)
    y_other(1, 1)
    p_hand_on(1)
    y_hand_on(0, 0)
    y_hand_on(0, 1)
    y_mine(1, 0)
    y_mine(1, 1)
    y_plain(1)
    p_sum(0)
    join_factors()
    p_sum(1)
    y_hand_on(1, 0)
    y_hand_on(1, 1)
    y_sum(0, 0)
    y_sum(0, 1)
    p_take(0)
    p_take(1)
    s_product()
    y_sum(1, 0)
    y_sum(1, 1)
    s_sum()
    z_start(0)
    z_start(1)
    p_correct()
    both(gather_z.hand_on, 0)
    gather_z.relay_pair()
    vv_tile(0)
    both(gather_p.hand_on, 0)
    gather_p.relay_pair()
    vv_tile(1)
    both(gather_z.take_near, 0)
    both(gather_z.hand_on, 1)
    vv_tile(2)
    both(gather_z.take_far, 0)
    both(gather_p.hand_on, 1)
    both(gather_z.take_near, 1)
    both(gather_z.take_far, 1)
    z_tile(0, 0)
    z_tile(0, 1)
    for q in range(2):
        for level in range(2):
            gather_z.take_core(level, q)
        z_tile(1, q)
    for level in range(2):
        both(gather_p.take_near, level)
        both(gather_p.take_far, level)

    for away, far in halves:
        pl.when(away)(far.wait_send)
    send.finish()
    landed(g_rx, g_s.at[0])
    landed(g_all.at[pl.ds(0, 15)], g_s.at[1])
    landed(s_rx, g_s.at[2])
    landed(s_rx, g_s.at[3])


def last(w, vv, p_all, out, done, sem):
    outs = []
    for i in range(6):
        rows = slice(i * 256, (i + 1) * 256)
        done[rows, :] = w[rows, :] - mm(vv[:, rows], p_all[...].reshape(512, 768), 0, 0)
        copy = pltpu.make_async_copy(done.at[pl.ds(i * 256, 256)], out.at[pl.ds(i * 256, 256)], sem.at[i])
        copy.start()
        outs.append(copy)
    for copy in outs:
        copy.wait()


def body(window, reflectors, factors):
    vt = jnp.swapaxes(reflectors, 1, 2)
    dma = pltpu.SemaphoreType.DMA
    vmem = lambda *s: pltpu.VMEM(s, F32)
    parts = pl.pallas_call(
        kernel,
        out_shape=[jax.ShapeDtypeStruct(q, F32) for q in ((1536, 768), (512, 1536), (2, 8, 32, 768))],
        in_specs=[pl.BlockSpec(memory_space=pltpu.HBM)] * 3,
        out_specs=[pl.BlockSpec(memory_space=pltpu.VMEM)] * 3,
        scratch_shapes=[
            vmem(2, 16, 16, 1536), vmem(2, 16, 16, 768), vmem(2, 256, 256), vmem(512, 512),
            vmem(2, 4, 2, 32, 768), vmem(2, 2, 32, 768), vmem(2, 4, 32, 768), vmem(2, 2, 32, 768),
            vmem(2, 32, 768), vmem(64, 768),
            vmem(2, 2, 384, 256), vmem(2, 2, 384, 256), vmem(2, 2, 4, 2, 48, 256), vmem(2, 2, 2, 48, 256),
            vmem(2, 2, 2, 2, 48, 256), vmem(2, 2, 2, 48, 256), vmem(2, 2, 48, 256), vmem(2, 2, 4, 2, 48, 512),
            vmem(16, 256), vmem(7, 16, 256), vmem(16, 256), vmem(16, 16, 256),
            vmem(2, 64, 256), vmem(15, 8, 256), vmem(8, 256), vmem(2, 64, 256),
            dma((3,)), dma((2, 2)), dma((2, 2)), dma((180,)), dma((2, 32)), dma((2, 16)), dma((16,)), dma((32,)),
            dma((2, 2)), dma((2, 4)), dma((2,)), dma((2, 2)), dma((2, 2)), dma((2, 2, 2)), dma((2, 2)),
            dma((4,)), dma((4,)),
        ],
        compiler_params=pltpu.CompilerParams(
            has_side_effects=True, collective_id=0, vmem_limit_bytes=40 * 1024 * 1024
        ),
    )(*(pltpu.with_memory_space_constraint(a, pltpu.HBM) for a in (window, vt, factors)))
    return pl.pallas_call(
        last,
        out_shape=jax.ShapeDtypeStruct(window.shape, F32),
        in_specs=[pl.BlockSpec(memory_space=pltpu.VMEM)] * 3,
        out_specs=pl.BlockSpec(memory_space=pl.ANY),
        scratch_shapes=[pltpu.VMEM(window.shape, F32), dma((6,))],
        compiler_params=pltpu.CompilerParams(vmem_limit_bytes=14 * 1024 * 1024),
    )(*parts)


def solution(mesh):
    placed = (P("row", "col"), P(None, "row", "col"), P())
    return jax.shard_map(body, mesh=mesh, in_specs=placed, out_specs=P("row", "col"), check_vma=False)
```
